512 devices in a mesh: stn: 64 (over x, z_hi, y), tm: 8 (over z_lo, core).
Axes of the slice: x: 4, y: 8, z: 8 (z_hi: 2, z_lo: 4; z = z_hi * 4 + z_lo), core: 2. Of those that a mesh axis runs over, the one named last changes fastest.
Arguments:
- samples: bfloat16 [256, 32768], P('stn', 'tm'), may hold values from -200 to 200
- array_sizes: int32 [64], replicated, may hold values from 1 to 4, as said below
- partner: int32 [64], replicated, may hold values from 0 to 63, as said below
Outputs:
- correlation: float32 [1024, 4096], P(('stn', 'tm'))
- residual: float32 [1024, 4096], P(('stn', 'tm'))
The draws below stay inside these ranges and needn't reach their ends.
Inputs may be any that keep to these rules, and one draw needn't show every extreme that they name: partner[i] = i XOR r for one round number r, 1 <= r < 64, the same for every i. Block i's live stations are its first array_sizes[i] slots.
All inputs are finite; a program needn't handle non-finite values.
Results may differ from the reference program's by a relative error of at most 0.0003.
Values may be sent and summed in bfloat16 or wider, within the bound.
A program may use at most 64 MiB of HBM per device.

```python
import math
import jax
import jax.numpy as jnp
from jax import lax

STN_DEV = 4
LAGS = 4096
SPECTRUM = 8192
BLOCKS = 64
STATIONS = 256
TIME = 32768
WINDOWS = 8
PAIRS = 1024


def draw_samples(key, part):
    noise_key = jax.random.fold_in(key, 11)
    scale_key = jax.random.fold_in(key, 12)
    noise = jnp.clip(jax.random.normal(noise_key, (STATIONS, TIME), jnp.float32), -6.0, 6.0)
    growth = math.log(3.0)
    station_scale = jnp.exp(jax.random.uniform(scale_key, (STATIONS, 1), jnp.float32, 0.0, math.log(10.0)))
    envelope = jnp.exp(growth * jnp.arange(TIME, dtype=jnp.float32) / TIME)[None, :]
    return (noise * station_scale * envelope).astype(jnp.bfloat16)


def draw_array_sizes(key, part):
    counts = jax.random.randint(jax.random.fold_in(key, 21), (BLOCKS,), 1, STN_DEV + 1)
    order = jax.random.permutation(jax.random.fold_in(key, 22), BLOCKS)
    counts = counts.at[order[0]].set(STN_DEV)
    counts = counts.at[order[1]].set(1)
    return counts.astype(jnp.int32)


def draw_partner(key, part):
    round_number = jax.random.randint(jax.random.fold_in(key, 31), (), 1, BLOCKS)
    return jnp.bitwise_xor(jnp.arange(BLOCKS, dtype=jnp.int32), round_number).astype(jnp.int32)


def setup_inputs(seed: int = 0) -> dict:
    splits = jax.random.split(jax.random.key(seed), 4)
    return {
        "samples": draw_samples(jax.random.fold_in(splits[3], 71), 0),
        "array_sizes": draw_array_sizes(jax.random.fold_in(splits[3], 71), 0),
        "partner": draw_partner(jax.random.fold_in(splits[3], 71), 0),
    }


small_term = 1e-06

def block_spectra(station_rows):
    count = station_rows.shape[0]
    padded = jnp.concatenate([station_rows, jnp.zeros((count, LAGS), station_rows.dtype)], axis=1)
    pieces = padded.reshape(count, WINDOWS + 1, LAGS)
    windows = jnp.concatenate([pieces[:, :-1], pieces[:, 1:]], axis=2)
    spectra = jnp.fft.fft(windows, axis=-1)
    power = lax.optimization_barrier(jnp.sum(jnp.real(spectra) ** 2 + jnp.imag(spectra) ** 2, axis=1))
    smooth = power
    for shift_by in (-2, -1, 1, 2):
        smooth = smooth + jnp.roll(power, shift_by, axis=1)
    level = smooth / 5.0 / WINDOWS + small_term
    whitened = spectra / jnp.sqrt(level)[:, None, :]
    return (whitened, power / level)

def one_block(block_id, samples, array_sizes, partner):
    other_id = partner[block_id]
    own_rows = lax.dynamic_slice(samples, ((block_id * STN_DEV).astype(jnp.int32), jnp.int32(0)), (STN_DEV, TIME)).astype(jnp.float32)
    far_rows = lax.dynamic_slice(samples, ((other_id * STN_DEV).astype(jnp.int32), jnp.int32(0)), (STN_DEV, TIME)).astype(jnp.float32)
    own_white, own_auto = block_spectra(own_rows)
    far_white, unused_auto = block_spectra(far_rows)
    cross = jnp.einsum('ajf,bjf->abf', jnp.conj(own_white), far_white, precision=lax.Precision.HIGHEST)
    ratio = own_auto / (lax.optimization_barrier(jnp.mean(own_auto, axis=1, keepdims=True)) + small_term)
    refined = cross * (1.0 - ratio)[:, None, :]
    factor = SPECTRUM / jnp.sqrt(jnp.float32(SPECTRUM * WINDOWS))
    plain_lags = jnp.real(jnp.fft.ifft(cross, axis=-1))[..., :LAGS] * factor
    refined_lags = jnp.real(jnp.fft.ifft(refined, axis=-1))[..., :LAGS] * factor
    slots = jnp.arange(STN_DEV, dtype=jnp.int32)
    live = ((slots[:, None] < array_sizes[block_id]) & (slots[None, :] < array_sizes[other_id])).astype(plain_lags.dtype)
    return (plain_lags * live[:, :, None], refined_lags * live[:, :, None])

def reference(samples, array_sizes, partner):

    def step_block(block_id):
        return one_block(block_id, samples, array_sizes, partner)
    plain_all, refined_all = lax.map(step_block, jnp.arange(BLOCKS, dtype=jnp.int32))
    return (plain_all.reshape(PAIRS, LAGS), refined_all.reshape(PAIRS, LAGS))
```

```python
import math

import jax
import jax.numpy as jnp
import ml_dtypes
import numpy as np
from jax import lax
from jax.experimental import pallas as pl
from jax.experimental.pallas import tpu as pltpu
from jax.sharding import PartitionSpec as P

LAGS = 4096
SPECTRUM = 8192
WINDOWS = 8
STN_DEV = 4
LINE = 8
LANES = 128
COARSE = 64
HALO = 2
ROWS = 40
N1_BLOCK = LAGS // LANES
REC_ROWS = (WINDOWS + 1) * N1_BLOCK
SMALL = 1e-06
F32 = jnp.float32
BF16 = jnp.bfloat16


def split_table(table):
    high = table.astype(ml_dtypes.bfloat16)
    low = (table - high.astype(np.float64)).astype(ml_dtypes.bfloat16)
    return high, low


def tables():
    f1 = np.arange(ROWS) - HALO
    n1 = np.arange(COARSE)
    n2 = np.arange(LANES)
    phase = 2.0 * np.pi * (np.outer(f1, n1) % COARSE) / COARSE
    first = np.concatenate([np.cos(phase), -np.sin(phase)], axis=0)
    first = np.concatenate(split_table(first), axis=1)
    phase = 2.0 * np.pi * np.outer(f1, n2) / SPECTRUM
    twist = np.concatenate([np.cos(phase), np.sin(phase)], axis=1).astype(np.float32)
    phase = 2.0 * np.pi * (np.outer(n2, n2) % LANES) / LANES
    cos, sin = np.cos(phase), np.sin(phase)
    second = np.block([[cos, -sin], [sin, cos]])
    second = np.concatenate(split_table(second), axis=1)
    weight = np.where((f1 == 0) | (f1 == COARSE // 2), 1.0, 2.0) * ((f1 >= 0) & (f1 <= COARSE // 2))
    lag1 = np.arange(N1_BLOCK)
    phase = 2.0 * np.pi * (np.outer(lag1, f1) % COARSE) / COARSE
    scale = 1.0 / math.sqrt(SPECTRUM * WINDOWS)
    last = np.concatenate([np.cos(phase) * weight, np.sin(phase) * weight], axis=1) * scale
    high, low = split_table(last)
    last = np.concatenate([high, low, high], axis=1)
    share = np.broadcast_to((weight / SPECTRUM)[:, None], (ROWS, LANES)).astype(np.float32)
    return first, twist, second, last, share


def halves(value):
    high = value.astype(BF16)
    low = (value - high.astype(F32)).astype(BF16)
    return high, low


def twisted(re, im, cos, sin):
    return re * cos + im * sin, im * cos - re * sin


def gather_kernel(own_ref, far_ref, out_ref, local_sem, send_sem, recv_sem):
    stn = lax.axis_index("stn")
    me = lax.axis_index("tm")
    barrier = pltpu.get_barrier_semaphore()
    for d in range(1, LINE):
        peer = lax.rem(me + d, LINE)
        pl.semaphore_signal(barrier, inc=1, device_id=(stn, peer), device_id_type=pl.DeviceIdType.MESH)
    my_rows = pl.ds(pl.multiple_of(me * N1_BLOCK, N1_BLOCK), N1_BLOCK)
    local = [
        pltpu.make_async_copy(own_ref.at[pl.ds(me // 2, 1)], out_ref.at[pl.ds(0, 1), my_rows], local_sem.at[0]),
        pltpu.make_async_copy(
            far_ref.at[pl.ds(lax.rem(me, 2) * 2, 2)], out_ref.at[pl.ds(1, 2), my_rows], local_sem.at[1]
        ),
    ]
    for copy in local:
        copy.start()
    out_ref[:, WINDOWS * N1_BLOCK :, :] = jnp.zeros((3, N1_BLOCK, LANES), BF16)
    pl.semaphore_wait(barrier, LINE - 1)
    copies = []
    for d in range(1, LINE):
        peer = lax.rem(me + d, LINE)
        for kind in (1, 0):
            if kind:
                src = far_ref.at[pl.ds(lax.rem(peer, 2) * 2, 2)]
                dst = out_ref.at[pl.ds(1, 2), my_rows]
            else:
                src = own_ref.at[pl.ds(peer // 2, 1)]
                dst = out_ref.at[pl.ds(0, 1), my_rows]
            copy = pltpu.make_async_remote_copy(
                src_ref=src,
                dst_ref=dst,
                send_sem=send_sem.at[kind, d],
                recv_sem=recv_sem.at[kind, d],
                device_id=(stn, peer),
                device_id_type=pl.DeviceIdType.MESH,
            )
            copy.start()
            copies.append(copy)
    for copy in local:
        copy.wait()
    for copy in copies:
        copy.wait()


def gather_line(own, far):
    return pl.pallas_call(
        gather_kernel,
        name="gather_line",
        out_shape=jax.ShapeDtypeStruct((3, REC_ROWS, LANES), BF16),
        in_specs=[pl.BlockSpec(memory_space=pltpu.VMEM)] * 2,
        out_specs=pl.BlockSpec(memory_space=pltpu.VMEM),
        scratch_shapes=[
            pltpu.SemaphoreType.DMA((2,)),
            pltpu.SemaphoreType.DMA((2, LINE)),
            pltpu.SemaphoreType.DMA((2, LINE)),
        ],
        compiler_params=pltpu.CompilerParams(collective_id=0, has_side_effects=True),
    )(own, far)


def correlate_kernel(
    sizes_ref, partner_ref, place_ref, rec_ref, first_ref, twist_ref, second_ref, last_ref, share_ref,
    plain_ref, refined_ref, left_ref, spec_ref,
):
    cos, sin = twist_ref[:, :LANES], twist_ref[:, LANES:]
    cos2, sin2 = jnp.concatenate([cos, cos], axis=0), jnp.concatenate([sin, sin], axis=0)
    first = first_ref[...]
    second_hi, second_lo = second_ref[:, : 2 * LANES], second_ref[:, 2 * LANES :]
    roots = []
    powers = []
    levels = []
    for s in range(3):
        for j in range(0, WINDOWS, 2):
            one = rec_ref[s, j * N1_BLOCK : (j + 2) * N1_BLOCK, :]
            two = rec_ref[s, (j + 1) * N1_BLOCK : (j + 3) * N1_BLOCK, :]
            both = jnp.concatenate([one, two], axis=1)
            grid = jnp.dot(first, jnp.concatenate([both, both], axis=0), preferred_element_type=F32)
            re = jnp.concatenate([grid[:ROWS, :LANES], grid[:ROWS, LANES:]], axis=0)
            im = jnp.concatenate([grid[ROWS:, :LANES], grid[ROWS:, LANES:]], axis=0)
            re, im = twisted(re, im, cos2, sin2)
            rows = slice((s * WINDOWS + j) * ROWS, (s * WINDOWS + j + 2) * ROWS)
            re_hi, re_lo = halves(re)
            im_hi, im_lo = halves(im)
            left_ref[rows, :] = jnp.concatenate([re_hi, im_hi, re_lo, im_lo], axis=1)
        rows = slice(s * WINDOWS * ROWS, (s + 1) * WINDOWS * ROWS)
        left_hi = left_ref[rows, : 2 * LANES]
        left_lo = left_ref[rows, 2 * LANES :]
        spec_ref[rows, :] = (
            jnp.dot(left_hi, second_hi, preferred_element_type=F32)
            + jnp.dot(left_lo, second_hi, preferred_element_type=F32)
            + jnp.dot(left_hi, second_lo, preferred_element_type=F32)
        )
        power = jnp.zeros((ROWS, LANES), F32)
        for j in range(WINDOWS):
            one = spec_ref[(s * WINDOWS + j) * ROWS : (s * WINDOWS + j + 1) * ROWS, :]
            one = one * one
            power = power + one[:, :LANES] + one[:, LANES:]
        smooth = power
        for shift in (-2, -1, 1, 2):
            smooth = smooth + pltpu.roll(power, shift % ROWS, axis=0)
        level = smooth / 5.0 / WINDOWS + SMALL
        roots.append(1.0 / jnp.sqrt(level))
        powers.append(power)
        levels.append(level)

    auto = powers[0] / levels[0]
    mean = jnp.sum(auto * share_ref[...])
    keep = 1.0 - auto / (mean + SMALL)

    cross = []
    sums = [[jnp.zeros((ROWS, LANES), F32) for _ in range(2)] for _ in range(2)]
    for j in range(WINDOWS):
        source = spec_ref[j * ROWS : (j + 1) * ROWS, :]
        a_re, a_im = source[:, :LANES] * roots[0], source[:, LANES:] * roots[0]
        for b in range(2):
            start = ((b + 1) * WINDOWS + j) * ROWS
            target = spec_ref[start : start + ROWS, :]
            b_re, b_im = target[:, :LANES] * roots[b + 1], target[:, LANES:] * roots[b + 1]
            sums[b][0] = sums[b][0] + (a_re * b_re + a_im * b_im)
            sums[b][1] = sums[b][1] + (a_im * b_re - a_re * b_im)
    for b in range(2):
        plain = jnp.concatenate(sums[b], axis=1)
        cross.append(plain)
        cross.append(plain * jnp.concatenate([keep, keep], axis=1))
    cross = jnp.concatenate(cross, axis=0)
    cross_hi, cross_lo = halves(cross)
    half = (
        jnp.dot(cross_hi, second_hi, preferred_element_type=F32)
        + jnp.dot(cross_lo, second_hi, preferred_element_type=F32)
        + jnp.dot(cross_hi, second_lo, preferred_element_type=F32)
    )
    columns = []
    for i in range(4):
        part = half[i * ROWS : (i + 1) * ROWS]
        re, im = twisted(part[:, :LANES], part[:, LANES:], cos, sin)
        columns.append(jnp.concatenate([re, im], axis=0))
    columns = jnp.concatenate(columns, axis=1)
    col_hi, col_lo = halves(columns)
    lags = jnp.dot(last_ref[...], jnp.concatenate([col_hi, col_hi, col_lo], axis=0), preferred_element_type=F32)

    block = place_ref[0]
    line = place_ref[1]
    source_live = (line // 2 < sizes_ref[block]).astype(F32)
    other_size = sizes_ref[partner_ref[block]]
    for b in range(2):
        live = source_live * (lax.rem(line, 2) * 2 + b < other_size).astype(F32)
        for kind, ref in enumerate((plain_ref, refined_ref)):
            index = 2 * b + kind
            value = lags[:, index * LANES : (index + 1) * LANES] * live
            for k in range(N1_BLOCK):
                ref[b : b + 1, k * LANES : (k + 1) * LANES] = value[k : k + 1, :]


def correlate(array_sizes, partner, place, record):
    out = jax.ShapeDtypeStruct((2, LAGS), F32)
    smem = pl.BlockSpec(memory_space=pltpu.SMEM)
    vmem = pl.BlockSpec(memory_space=pltpu.VMEM)
    return pl.pallas_call(
        correlate_kernel,
        name="correlate",
        out_shape=(out, out),
        in_specs=[smem] * 3 + [vmem] * 6,
        out_specs=(vmem, vmem),
        scratch_shapes=[
            pltpu.VMEM((3 * WINDOWS * ROWS, 4 * LANES), BF16),
            pltpu.VMEM((3 * WINDOWS * ROWS, 2 * LANES), F32),
        ],
    )(array_sizes, partner, place, record, *(jnp.asarray(table) for table in tables()))


def per_device(samples, array_sizes, partner):
    count = lax.axis_size("stn")
    own = samples.reshape(STN_DEV, N1_BLOCK, LANES)

    def moved(round_number):
        return lambda rows: lax.ppermute(rows, "stn", [(i, i ^ round_number) for i in range(count)])

    far = lax.switch(partner[0] - 1, [moved(r) for r in range(1, count)], own)
    record = gather_line(own, far)
    place = jnp.stack([lax.axis_index("stn"), lax.axis_index("tm")]).astype(jnp.int32)
    return correlate(array_sizes, partner, place, record)


def solution(mesh):
    placed = (P("stn", "tm"), P(), P())
    return jax.shard_map(
        per_device,
        mesh=mesh,
        in_specs=placed,
        out_specs=(P(("stn", "tm"), None), P(("stn", "tm"), None)),
        check_vma=False,
    )
```

```python
import functools
import math

import jax
import jax.numpy as jnp
import ml_dtypes
import numpy as np
from jax import lax
from jax.experimental import pallas as pl
from jax.experimental.pallas import tpu as pltpu
from jax.sharding import PartitionSpec as P

LAGS = 4096
SPECTRUM = 8192
WINDOWS = 8
STN_DEV = 4
LINE = 8
LANES = 128
COARSE = 64
HALO = 2
ROWS = 40
N1_BLOCK = LAGS // LANES
REC_ROWS = (WINDOWS + 1) * N1_BLOCK
SMALL = 1e-06
F32 = jnp.float32
BF16 = jnp.bfloat16


def split_table(table):
    high = table.astype(ml_dtypes.bfloat16)
    low = (table - high.astype(np.float64)).astype(ml_dtypes.bfloat16)
    return high, low


def tables():
    f1 = np.arange(ROWS) - HALO
    n1 = np.arange(COARSE)
    n2 = np.arange(LANES)
    phase = 2.0 * np.pi * (np.outer(f1, n1) % COARSE) / COARSE
    first = np.concatenate([np.cos(phase), -np.sin(phase)], axis=0)
    first = np.concatenate(split_table(first), axis=1)
    phase = 2.0 * np.pi * np.outer(f1, n2) / SPECTRUM
    twist = np.concatenate([np.cos(phase), np.sin(phase)], axis=1).astype(np.float32)
    phase = 2.0 * np.pi * (np.outer(n2, n2) % LANES) / LANES
    cos, sin = np.cos(phase), np.sin(phase)
    second = np.block([[cos, -sin], [sin, cos]])
    second = np.concatenate(split_table(second), axis=1)
    weight = np.where((f1 == 0) | (f1 == COARSE // 2), 1.0, 2.0) * ((f1 >= 0) & (f1 <= COARSE // 2))
    lag1 = np.arange(N1_BLOCK)
    phase = 2.0 * np.pi * (np.outer(lag1, f1) % COARSE) / COARSE
    scale = 1.0 / math.sqrt(SPECTRUM * WINDOWS)
    last = np.concatenate([np.cos(phase) * weight, np.sin(phase) * weight], axis=1) * scale
    high, low = split_table(last)
    last = np.concatenate([high, low, high], axis=1)
    share = np.broadcast_to((weight / SPECTRUM)[:, None], (ROWS, LANES)).astype(np.float32)
    return first, twist, second, last, share


def halves(value):
    high = value.astype(BF16)
    low = (value - high.astype(F32)).astype(BF16)
    return high, low


def twisted(re, im, cos, sin):
    return re * cos + im * sin, im * cos - re * sin


def exchange_kernel(
    high, partner_ref, samples_ref, out_ref, rows_ref, own_ref, pair_ref, far_ref, local_sem, pair_send, pair_recv, send_sem, recv_sem
):
    stn = lax.axis_index("stn")
    me = lax.axis_index("tm")
    barrier = pltpu.get_barrier_semaphore()
    others = [(stn ^ (2 * high + low), me) for low in range(2) if 2 * high + low]
    line = [(stn, lax.rem(me + d, LINE)) for d in range(1, LINE)]
    for device in others + line:
        pl.semaphore_signal(barrier, inc=1, device_id=device, device_id_type=pl.DeviceIdType.MESH)
    for k in range(N1_BLOCK):
        piece = samples_ref[:, k * LANES : (k + 1) * LANES].astype(F32)
        for s in range(STN_DEV):
            rows_ref[s, k : k + 1, :] = piece[s : s + 1, :]
    own_ref[...] = rows_ref[...].astype(BF16)
    my_rows = pl.ds(pl.multiple_of(me * N1_BLOCK, N1_BLOCK), N1_BLOCK)
    pl.semaphore_wait(barrier, len(others + line))

    def remote(src, dst, send, recv, device):
        copy = pltpu.make_async_remote_copy(
            src_ref=src, dst_ref=dst, send_sem=send, recv_sem=recv, device_id=device, device_id_type=pl.DeviceIdType.MESH
        )
        copy.start()
        return copy

    swaps = []
    for i, device in enumerate(others, 2 - len(others)):
        swaps.append(remote(own_ref, pair_ref.at[i], pair_send.at[i], pair_recv.at[i], device))
    copies = []
    for d, device in enumerate(line, 1):
        copies.append(
            remote(
                own_ref.at[pl.ds(device[1] // 2, 1)], out_ref.at[pl.ds(0, 1), my_rows], send_sem.at[0, d], recv_sem.at[0, d], device
            )
        )
    local = [pltpu.make_async_copy(own_ref.at[pl.ds(me // 2, 1)], out_ref.at[pl.ds(0, 1), my_rows], local_sem.at[0])]
    local[0].start()
    out_ref[:, WINDOWS * N1_BLOCK :, :] = jnp.zeros((3, N1_BLOCK, LANES), BF16)
    for copy in swaps:
        copy.wait()
    far_ref[...] = pair_ref[jnp.bitwise_and(partner_ref[0], 1)] if high else pair_ref[1]
    for d, device in enumerate(line, 1):
        copies.append(
            remote(
                far_ref.at[pl.ds(lax.rem(device[1], 2) * 2, 2)],
                out_ref.at[pl.ds(1, 2), my_rows],
                send_sem.at[1, d],
                recv_sem.at[1, d],
                device,
            )
        )
    local.append(
        pltpu.make_async_copy(far_ref.at[pl.ds(lax.rem(me, 2) * 2, 2)], out_ref.at[pl.ds(1, 2), my_rows], local_sem.at[1])
    )
    local[1].start()
    for copy in local + copies:
        copy.wait()


def exchange(high, samples, partner):
    block = (STN_DEV, N1_BLOCK, LANES)
    return pl.pallas_call(
        functools.partial(exchange_kernel, high),
        name="exchange",
        out_shape=jax.ShapeDtypeStruct((3, REC_ROWS, LANES), BF16),
        in_specs=[pl.BlockSpec(memory_space=pltpu.SMEM), pl.BlockSpec(memory_space=pltpu.VMEM)],
        out_specs=pl.BlockSpec(memory_space=pltpu.VMEM),
        scratch_shapes=[
            pltpu.VMEM(block, F32),
            pltpu.VMEM(block, BF16),
            pltpu.VMEM((2,) + block, BF16),
            pltpu.VMEM(block, BF16),
            pltpu.SemaphoreType.DMA((2,)),
            pltpu.SemaphoreType.DMA((2,)),
            pltpu.SemaphoreType.DMA((2,)),
            pltpu.SemaphoreType.DMA((2, LINE)),
            pltpu.SemaphoreType.DMA((2, LINE)),
        ],
        compiler_params=pltpu.CompilerParams(collective_id=high, has_side_effects=True),
    )(partner, samples)


def correlate_kernel(
    sizes_ref, partner_ref, rec_ref, first_ref, twist_ref, second_ref, last_ref, share_ref,
    plain_ref, refined_ref, left_ref, spec_ref,
):
    cos, sin = twist_ref[:, :LANES], twist_ref[:, LANES:]
    cos2, sin2 = jnp.concatenate([cos, cos], axis=0), jnp.concatenate([sin, sin], axis=0)
    first = first_ref[...]
    second_hi, second_lo = second_ref[:, : 2 * LANES], second_ref[:, 2 * LANES :]
    roots = []
    powers = []
    levels = []
    for s in range(3):
        for j in range(0, WINDOWS, 2):
            one = rec_ref[s, j * N1_BLOCK : (j + 2) * N1_BLOCK, :]
            two = rec_ref[s, (j + 1) * N1_BLOCK : (j + 3) * N1_BLOCK, :]
            both = jnp.concatenate([one, two], axis=1)
            grid = jnp.dot(first, jnp.concatenate([both, both], axis=0), preferred_element_type=F32)
            re = jnp.concatenate([grid[:ROWS, :LANES], grid[:ROWS, LANES:]], axis=0)
            im = jnp.concatenate([grid[ROWS:, :LANES], grid[ROWS:, LANES:]], axis=0)
            re, im = twisted(re, im, cos2, sin2)
            rows = slice((s * WINDOWS + j) * ROWS, (s * WINDOWS + j + 2) * ROWS)
            re_hi, re_lo = halves(re)
            im_hi, im_lo = halves(im)
            left_ref[rows, :] = jnp.concatenate([re_hi, im_hi, re_lo, im_lo], axis=1)
        rows = slice(s * WINDOWS * ROWS, (s + 1) * WINDOWS * ROWS)
        left_hi = left_ref[rows, : 2 * LANES]
        left_lo = left_ref[rows, 2 * LANES :]
        spec_ref[rows, :] = (
            jnp.dot(left_hi, second_hi, preferred_element_type=F32)
            + jnp.dot(left_lo, second_hi, preferred_element_type=F32)
            + jnp.dot(left_hi, second_lo, preferred_element_type=F32)
        )
        power = jnp.zeros((ROWS, LANES), F32)
        for j in range(WINDOWS):
            one = spec_ref[(s * WINDOWS + j) * ROWS : (s * WINDOWS + j + 1) * ROWS, :]
            one = one * one
            power = power + one[:, :LANES] + one[:, LANES:]
        smooth = power
        for shift in (-2, -1, 1, 2):
            smooth = smooth + pltpu.roll(power, shift % ROWS, axis=0)
        level = smooth / 5.0 / WINDOWS + SMALL
        roots.append(1.0 / jnp.sqrt(level))
        powers.append(power)
        levels.append(level)

    auto = powers[0] / levels[0]
    mean = jnp.sum(auto * share_ref[...])
    keep = 1.0 - auto / (mean + SMALL)

    cross = []
    sums = [[jnp.zeros((ROWS, LANES), F32) for _ in range(2)] for _ in range(2)]
    for j in range(WINDOWS):
        source = spec_ref[j * ROWS : (j + 1) * ROWS, :]
        a_re, a_im = source[:, :LANES] * roots[0], source[:, LANES:] * roots[0]
        for b in range(2):
            start = ((b + 1) * WINDOWS + j) * ROWS
            target = spec_ref[start : start + ROWS, :]
            b_re, b_im = target[:, :LANES] * roots[b + 1], target[:, LANES:] * roots[b + 1]
            sums[b][0] = sums[b][0] + (a_re * b_re + a_im * b_im)
            sums[b][1] = sums[b][1] + (a_im * b_re - a_re * b_im)
    for b in range(2):
        plain = jnp.concatenate(sums[b], axis=1)
        cross.append(plain)
        cross.append(plain * jnp.concatenate([keep, keep], axis=1))
    cross = jnp.concatenate(cross, axis=0)
    cross_hi, cross_lo = halves(cross)
    half = (
        jnp.dot(cross_hi, second_hi, preferred_element_type=F32)
        + jnp.dot(cross_lo, second_hi, preferred_element_type=F32)
        + jnp.dot(cross_hi, second_lo, preferred_element_type=F32)
    )
    columns = []
    for i in range(4):
        part = half[i * ROWS : (i + 1) * ROWS]
        re, im = twisted(part[:, :LANES], part[:, LANES:], cos, sin)
        columns.append(jnp.concatenate([re, im], axis=0))
    columns = jnp.concatenate(columns, axis=1)
    col_hi, col_lo = halves(columns)
    lags = jnp.dot(last_ref[...], jnp.concatenate([col_hi, col_hi, col_lo], axis=0), preferred_element_type=F32)

    block = lax.axis_index("stn")
    line = lax.axis_index("tm")
    source_live = (line // 2 < sizes_ref[block]).astype(F32)
    other_size = sizes_ref[partner_ref[block]]
    for b in range(2):
        live = source_live * (lax.rem(line, 2) * 2 + b < other_size).astype(F32)
        for kind, ref in enumerate((plain_ref, refined_ref)):
            index = 2 * b + kind
            value = lags[:, index * LANES : (index + 1) * LANES] * live
            for k in range(N1_BLOCK):
                ref[b : b + 1, k * LANES : (k + 1) * LANES] = value[k : k + 1, :]


def correlate(array_sizes, partner, record):
    out = jax.ShapeDtypeStruct((2, LAGS), F32)
    smem = pl.BlockSpec(memory_space=pltpu.SMEM)
    vmem = pl.BlockSpec(memory_space=pltpu.VMEM)
    return pl.pallas_call(
        correlate_kernel,
        name="correlate",
        out_shape=(out, out),
        in_specs=[smem] * 2 + [vmem] * 6,
        out_specs=(vmem, vmem),
        scratch_shapes=[
            pltpu.VMEM((3 * WINDOWS * ROWS, 4 * LANES), BF16),
            pltpu.VMEM((3 * WINDOWS * ROWS, 2 * LANES), F32),
        ],
    )(array_sizes, partner, record, *(jnp.asarray(table) for table in tables()))


def per_device(samples, array_sizes, partner):
    branches = [functools.partial(exchange, high) for high in range(lax.axis_size("stn") // 2)]
    record = lax.switch(lax.shift_right_logical(partner[0], 1), branches, samples, partner)
    return correlate(array_sizes, partner, record)


def solution(mesh):
    placed = (P("stn", "tm"), P(), P())
    return jax.shard_map(
        per_device,
        mesh=mesh,
        in_specs=placed,
        out_specs=(P(("stn", "tm"), None), P(("stn", "tm"), None)),
        check_vma=False,
    )
```

```python
import functools
import math

import jax
import jax.numpy as jnp
import ml_dtypes
import numpy as np
from jax import lax
from jax.experimental import pallas as pl
from jax.experimental.pallas import tpu as pltpu
from jax.sharding import PartitionSpec as P

LAGS = 4096
SPECTRUM = 8192
WINDOWS = 8
STN_DEV = 4
LINE = 8
LANES = 128
COARSE = 64
HALO = 2
ROWS = 40
N1_BLOCK = LAGS // LANES
REC_ROWS = (WINDOWS + 1) * N1_BLOCK
SMALL = 1e-06
F32 = jnp.float32
BF16 = jnp.bfloat16


def split_table(table):
    high = table.astype(ml_dtypes.bfloat16)
    low = (table - high.astype(np.float64)).astype(ml_dtypes.bfloat16)
    return high, low


def tables():
    f1 = np.arange(ROWS) - HALO
    n1 = np.arange(COARSE)
    n2 = np.arange(LANES)
    phase = 2.0 * np.pi * (np.outer(f1, n1) % COARSE) / COARSE
    first = np.concatenate([np.cos(phase), -np.sin(phase)], axis=0)
    first = np.concatenate(split_table(first), axis=1)
    phase = 2.0 * np.pi * np.outer(f1, n2) / SPECTRUM
    twist = np.concatenate([np.cos(phase), np.sin(phase)], axis=1).astype(np.float32)
    phase = 2.0 * np.pi * (np.outer(n2, n2) % LANES) / LANES
    cos, sin = np.cos(phase), np.sin(phase)
    second = np.block([[cos, -sin], [sin, cos]])
    second = np.concatenate(split_table(second), axis=1)
    weight = np.where((f1 == 0) | (f1 == COARSE // 2), 1.0, 2.0) * ((f1 >= 0) & (f1 <= COARSE // 2))
    lag1 = np.arange(N1_BLOCK)
    phase = 2.0 * np.pi * (np.outer(lag1, f1) % COARSE) / COARSE
    scale = 1.0 / math.sqrt(SPECTRUM * WINDOWS)
    last = np.concatenate([np.cos(phase) * weight, np.sin(phase) * weight], axis=1) * scale
    high, low = split_table(last)
    last = np.concatenate([high, low, high], axis=1)
    share = np.broadcast_to((weight / SPECTRUM)[:, None], (ROWS, LANES)).astype(np.float32)
    return first, twist, second, last, share


def halves(value):
    high = value.astype(BF16)
    low = (value - high.astype(F32)).astype(BF16)
    return high, low


def twisted(re, im, cos, sin):
    return re * cos + im * sin, im * cos - re * sin


def remote(src, dst, send, recv, device):
    return pltpu.make_async_remote_copy(
        src_ref=src, dst_ref=dst, send_sem=send, recv_sem=recv, device_id=device, device_id_type=pl.DeviceIdType.MESH
    )


def signal(semaphore, device):
    pl.semaphore_signal(semaphore, inc=1, device_id=device, device_id_type=pl.DeviceIdType.MESH)


def exchange_kernel(high, n_tables, partner_ref, samples_ref, *refs):
    tables_in, out_ref, tables_out = refs[:n_tables], refs[n_tables], refs[n_tables + 1 : 2 * n_tables + 1]
    (
        partner_smem, samples_vmem, rows_ref, own_ref, pair_ref, in_sem, table_sem, pair_send, pair_recv, own_send, own_recv, far_send,
        far_recv,
    ) = refs[2 * n_tables + 1 :]
    stn = lax.axis_index("stn")
    me = lax.axis_index("tm")
    chip, core = me // 2, lax.rem(me, 2)
    barrier = pltpu.get_barrier_semaphore()
    lows = range(0 if high else 1, 2)
    others = [(low, to, (stn ^ (2 * high + low), 2 * chip + to)) for low in lows for to in range(2)]
    line = [lax.rem(me + d, LINE) for d in range(1, LINE)]
    for device in [device for _, _, device in others] + [(stn, peer) for peer in line]:
        signal(barrier, device)
    loads = [
        pltpu.make_async_copy(samples_ref, samples_vmem, in_sem.at[0]),
        pltpu.make_async_copy(partner_ref, partner_smem, in_sem.at[1]),
    ]
    fetches = [pltpu.make_async_copy(a, b, table_sem.at[i]) for i, (a, b) in enumerate(zip(tables_in, tables_out))]
    for copy in loads + fetches:
        copy.start()
    loads[0].wait()
    for k in range(N1_BLOCK):
        piece = samples_vmem[:, k * LANES : (k + 1) * LANES].astype(F32)
        for s in range(STN_DEV):
            rows_ref[s, k : k + 1, :] = piece[s : s + 1, :]
    own_ref[...] = rows_ref[...].astype(BF16)
    pl.semaphore_wait(barrier, len(others) + len(line))

    my_rows = pl.ds(pl.multiple_of(me * N1_BLOCK, N1_BLOCK), N1_BLOCK)
    chip_rows = pl.ds(pl.multiple_of(chip * 2 * N1_BLOCK, 2 * N1_BLOCK), 2 * N1_BLOCK)
    core_rows = pl.ds(pl.multiple_of(core * N1_BLOCK, N1_BLOCK), N1_BLOCK)
    swaps = [
        remote(own_ref.at[pl.ds(2 * to, 2)], pair_ref.at[low, :, core_rows], pair_send.at[low, to], pair_recv.at[low, core], device)
        for low, to, device in others
    ]
    arrivals = [
        remote(own_ref.at[pl.ds(0, 2)], pair_ref.at[low, :, pl.ds(to * N1_BLOCK, N1_BLOCK)], pair_send.at[low, to], pair_recv.at[low, to], device)
        for low, to, device in others
    ]
    for copy in swaps:
        copy.start()
    copies = []
    for d, peer in enumerate(line):
        copy = remote(
            own_ref.at[pl.ds(peer // 2, 1)], out_ref.at[pl.ds(0, 1), my_rows], own_send.at[d], own_recv.at[d], (stn, peer)
        )
        copy.start()
        copies.append(copy)
    out_ref[0, my_rows, :] = own_ref[chip]
    out_ref[:, WINDOWS * N1_BLOCK :, :] = jnp.zeros((3, N1_BLOCK, LANES), BF16)
    loads[1].wait()
    for copy in arrivals:
        copy.wait_recv()
    out_ref[1:3, chip_rows, :] = pair_ref[jnp.bitwise_and(partner_smem[0], 1)] if high else pair_ref[1]
    for d in range(LINE // 2 - 1):
        peer = lax.rem(me + 2 * (d + 1), LINE)
        copy = remote(
            out_ref.at[pl.ds(1, 2), chip_rows], out_ref.at[pl.ds(1, 2), chip_rows], far_send.at[d], far_recv.at[d], (stn, peer)
        )
        copy.start()
        copies.append(copy)
    for copy in copies:
        copy.wait_recv()
    for copy in copies + swaps:
        copy.wait_send()
    for copy in fetches:
        copy.wait()


def exchange(high, samples, partner, *consts):
    block = (STN_DEV, N1_BLOCK, LANES)
    anywhere = pl.BlockSpec(memory_space=pl.ANY)
    vmem = pl.BlockSpec(memory_space=pltpu.VMEM)
    return pl.pallas_call(
        functools.partial(exchange_kernel, high, len(consts)),
        name="exchange",
        out_shape=(jax.ShapeDtypeStruct((3, REC_ROWS, LANES), BF16),)
        + tuple(jax.ShapeDtypeStruct(c.shape, c.dtype) for c in consts),
        in_specs=[anywhere] * (2 + len(consts)),
        out_specs=(vmem,) * (1 + len(consts)),
        scratch_shapes=[
            pltpu.SMEM(partner.shape, jnp.int32),
            pltpu.VMEM(samples.shape, BF16),
            pltpu.VMEM(block, F32),
            pltpu.VMEM(block, BF16),
            pltpu.VMEM((2, 2, 2 * N1_BLOCK, LANES), BF16),
            pltpu.SemaphoreType.DMA((2,)),
            pltpu.SemaphoreType.DMA((len(consts),)),
            pltpu.SemaphoreType.DMA((2, 2)),
            pltpu.SemaphoreType.DMA((2, 2)),
            pltpu.SemaphoreType.DMA((LINE - 1,)),
            pltpu.SemaphoreType.DMA((LINE - 1,)),
            pltpu.SemaphoreType.DMA((LINE // 2 - 1,)),
            pltpu.SemaphoreType.DMA((LINE // 2 - 1,)),
        ],
        compiler_params=pltpu.CompilerParams(collective_id=high, has_side_effects=True),
    )(partner, samples, *consts)


def correlate_kernel(
    sizes_ref, partner_ref, rec_ref, first_ref, twist_ref, second_ref, last_ref, share_ref,
    plain_ref, refined_ref, left_ref, spec_ref,
):
    cos, sin = twist_ref[:, :LANES], twist_ref[:, LANES:]
    cos2, sin2 = jnp.concatenate([cos, cos], axis=0), jnp.concatenate([sin, sin], axis=0)
    first = first_ref[...]
    second_hi, second_lo = second_ref[:, : 2 * LANES], second_ref[:, 2 * LANES :]
    roots = []
    powers = []
    levels = []
    for s in range(3):
        for j in range(0, WINDOWS, 2):
            one = rec_ref[s, j * N1_BLOCK : (j + 2) * N1_BLOCK, :]
            two = rec_ref[s, (j + 1) * N1_BLOCK : (j + 3) * N1_BLOCK, :]
            both = jnp.concatenate([one, two], axis=1)
            grid = jnp.dot(first, jnp.concatenate([both, both], axis=0), preferred_element_type=F32)
            re = jnp.concatenate([grid[:ROWS, :LANES], grid[:ROWS, LANES:]], axis=0)
            im = jnp.concatenate([grid[ROWS:, :LANES], grid[ROWS:, LANES:]], axis=0)
            re, im = twisted(re, im, cos2, sin2)
            rows = slice((s * WINDOWS + j) * ROWS, (s * WINDOWS + j + 2) * ROWS)
            re_hi, re_lo = halves(re)
            im_hi, im_lo = halves(im)
            left_ref[rows, :] = jnp.concatenate([re_hi, im_hi, re_lo, im_lo], axis=1)
        rows = slice(s * WINDOWS * ROWS, (s + 1) * WINDOWS * ROWS)
        left_hi = left_ref[rows, : 2 * LANES]
        left_lo = left_ref[rows, 2 * LANES :]
        spec_ref[rows, :] = (
            jnp.dot(left_hi, second_hi, preferred_element_type=F32)
            + jnp.dot(left_lo, second_hi, preferred_element_type=F32)
            + jnp.dot(left_hi, second_lo, preferred_element_type=F32)
        )
        power = jnp.zeros((ROWS, LANES), F32)
        for j in range(WINDOWS):
            one = spec_ref[(s * WINDOWS + j) * ROWS : (s * WINDOWS + j + 1) * ROWS, :]
            one = one * one
            power = power + one[:, :LANES] + one[:, LANES:]
        smooth = power
        for shift in (-2, -1, 1, 2):
            smooth = smooth + pltpu.roll(power, shift % ROWS, axis=0)
        level = smooth / 5.0 / WINDOWS + SMALL
        roots.append(1.0 / jnp.sqrt(level))
        powers.append(power)
        levels.append(level)

    auto = powers[0] / levels[0]
    mean = jnp.sum(auto * share_ref[...])
    keep = 1.0 - auto / (mean + SMALL)

    cross = []
    sums = [[jnp.zeros((ROWS, LANES), F32) for _ in range(2)] for _ in range(2)]
    for j in range(WINDOWS):
        source = spec_ref[j * ROWS : (j + 1) * ROWS, :]
        a_re, a_im = source[:, :LANES] * roots[0], source[:, LANES:] * roots[0]
        for b in range(2):
            start = ((b + 1) * WINDOWS + j) * ROWS
            target = spec_ref[start : start + ROWS, :]
            b_re, b_im = target[:, :LANES] * roots[b + 1], target[:, LANES:] * roots[b + 1]
            sums[b][0] = sums[b][0] + (a_re * b_re + a_im * b_im)
            sums[b][1] = sums[b][1] + (a_im * b_re - a_re * b_im)
    for b in range(2):
        plain = jnp.concatenate(sums[b], axis=1)
        cross.append(plain)
        cross.append(plain * jnp.concatenate([keep, keep], axis=1))
    cross = jnp.concatenate(cross, axis=0)
    cross_hi, cross_lo = halves(cross)
    half = (
        jnp.dot(cross_hi, second_hi, preferred_element_type=F32)
        + jnp.dot(cross_lo, second_hi, preferred_element_type=F32)
        + jnp.dot(cross_hi, second_lo, preferred_element_type=F32)
    )
    columns = []
    for i in range(4):
        part = half[i * ROWS : (i + 1) * ROWS]
        re, im = twisted(part[:, :LANES], part[:, LANES:], cos, sin)
        columns.append(jnp.concatenate([re, im], axis=0))
    columns = jnp.concatenate(columns, axis=1)
    col_hi, col_lo = halves(columns)
    lags = jnp.dot(last_ref[...], jnp.concatenate([col_hi, col_hi, col_lo], axis=0), preferred_element_type=F32)

    block = lax.axis_index("stn")
    line = lax.axis_index("tm")
    source_live = (line // 2 < sizes_ref[block]).astype(F32)
    other_size = sizes_ref[partner_ref[block]]
    for b in range(2):
        live = source_live * (lax.rem(line, 2) * 2 + b < other_size).astype(F32)
        for kind, ref in enumerate((plain_ref, refined_ref)):
            index = 2 * b + kind
            value = lags[:, index * LANES : (index + 1) * LANES] * live
            for k in range(N1_BLOCK):
                ref[b : b + 1, k * LANES : (k + 1) * LANES] = value[k : k + 1, :]


def correlate(array_sizes, partner, record, *consts):
    out = jax.ShapeDtypeStruct((2, LAGS), F32)
    smem = pl.BlockSpec(memory_space=pltpu.SMEM)
    vmem = pl.BlockSpec(memory_space=pltpu.VMEM)
    return pl.pallas_call(
        correlate_kernel,
        name="correlate",
        out_shape=(out, out),
        in_specs=[smem] * 2 + [vmem] * 6,
        out_specs=(vmem, vmem),
        scratch_shapes=[
            pltpu.VMEM((3 * WINDOWS * ROWS, 4 * LANES), BF16),
            pltpu.VMEM((3 * WINDOWS * ROWS, 2 * LANES), F32),
        ],
    )(array_sizes, partner, record, *consts)


def per_device(samples, array_sizes, partner):
    branches = [functools.partial(exchange, high) for high in range(lax.axis_size("stn") // 2)]
    consts = [jnp.asarray(table) for table in tables()]
    staged = lax.switch(lax.shift_right_logical(partner[0], 1), branches, samples, partner, *consts)
    return correlate(array_sizes, partner, *staged)


def solution(mesh):
    placed = (P("stn", "tm"), P(), P())
    return jax.shard_map(
        per_device,
        mesh=mesh,
        in_specs=placed,
        out_specs=(P(("stn", "tm"), None), P(("stn", "tm"), None)),
        check_vma=False,
    )
```

```python
import functools
import math

import jax
import jax.numpy as jnp
import ml_dtypes
import numpy as np
from jax import lax
from jax.experimental import pallas as pl
from jax.experimental.pallas import tpu as pltpu
from jax.sharding import PartitionSpec as P

LAGS = 4096
SPECTRUM = 8192
WINDOWS = 8
STN_DEV = 4
LINE = 8
LANES = 128
COARSE = 64
HALO = 2
ROWS = 40
N1_BLOCK = LAGS // LANES
HALF = N1_BLOCK // 2
REC_ROWS = (WINDOWS + 1) * N1_BLOCK
SMALL = 1e-06
F32 = jnp.float32
BF16 = jnp.bfloat16


def split_table(table):
    high = table.astype(ml_dtypes.bfloat16)
    low = (table - high.astype(np.float64)).astype(ml_dtypes.bfloat16)
    return high, low


def tables():
    f1 = np.arange(ROWS) - HALO
    n1 = np.arange(COARSE)
    n2 = np.arange(LANES)
    phase = 2.0 * np.pi * (np.outer(f1, n1) % COARSE) / COARSE
    first = np.concatenate([np.cos(phase), -np.sin(phase)], axis=0)
    first = np.concatenate(split_table(first), axis=1)
    phase = 2.0 * np.pi * np.outer(f1, n2) / SPECTRUM
    twist = np.concatenate([np.cos(phase), np.sin(phase)], axis=1).astype(np.float32)
    phase = 2.0 * np.pi * (np.outer(n2, n2) % LANES) / LANES
    cos, sin = np.cos(phase), np.sin(phase)
    second = np.block([[cos, -sin], [sin, cos]])
    second = np.concatenate(split_table(second), axis=1)
    weight = np.where((f1 == 0) | (f1 == COARSE // 2), 1.0, 2.0) * ((f1 >= 0) & (f1 <= COARSE // 2))
    lag1 = np.arange(N1_BLOCK)
    phase = 2.0 * np.pi * (np.outer(lag1, f1) % COARSE) / COARSE
    scale = 1.0 / math.sqrt(SPECTRUM * WINDOWS)
    last = np.concatenate([np.cos(phase) * weight, np.sin(phase) * weight], axis=1) * scale
    high, low = split_table(last)
    last = np.concatenate([high, low, high], axis=1)
    share = np.broadcast_to((weight / SPECTRUM)[:, None], (ROWS, LANES)).astype(np.float32)
    return first, twist, second, last, share


def halves(value):
    high = value.astype(BF16)
    low = (value - high.astype(F32)).astype(BF16)
    return high, low


def twisted(re, im, cos, sin):
    return re * cos + im * sin, im * cos - re * sin


def remote(src, dst, send, recv, device):
    return pltpu.make_async_remote_copy(
        src_ref=src, dst_ref=dst, send_sem=send, recv_sem=recv, device_id=device, device_id_type=pl.DeviceIdType.MESH
    )


def signal(semaphore, device):
    pl.semaphore_signal(semaphore, inc=1, device_id=device, device_id_type=pl.DeviceIdType.MESH)


def exchange_kernel(high, n_tables, partner_ref, samples_ref, *refs):
    tables_in, out_ref, tables_out = refs[:n_tables], refs[n_tables], refs[n_tables + 1 : 2 * n_tables + 1]
    (
        partner_smem, samples_vmem, rows_ref, own_ref, pair_ref, pick_ref, land_ref, in_sem, table_sem, pair_send, pair_recv, own_send, own_recv, far_send,
        far_recv,
    ) = refs[2 * n_tables + 1 :]
    stn = lax.axis_index("stn")
    me = lax.axis_index("tm")
    chip, core = me // 2, lax.rem(me, 2)
    barrier = pltpu.get_barrier_semaphore()
    others = [(low, to, (stn ^ (2 * high + low), 2 * chip + to)) for low in range(2) for to in range(2)]
    if not high:
        others = others[2:]
    line = [lax.rem(me + d, LINE) for d in range(1, LINE)]
    column = [lax.rem(me + 2 * d, LINE) for d in range(LINE // 2)]
    mate = me + 1 - 2 * core
    near = [device for _, _, device in others] + [(stn, peer) for peer in line]
    near += [(stn ^ 1, peer) for peer in (column if high else column[1:])]
    for device in near:
        signal(barrier, device)
    loads = [
        pltpu.make_async_copy(samples_ref, samples_vmem, in_sem.at[0]),
        pltpu.make_async_copy(partner_ref, partner_smem, in_sem.at[1]),
    ]
    fetches = [pltpu.make_async_copy(a, b, table_sem.at[i]) for i, (a, b) in enumerate(zip(tables_in, tables_out))]
    for copy in loads + fetches:
        copy.start()
    loads[0].wait()

    @pl.loop(0, N1_BLOCK)
    def _(k):
        piece = samples_vmem[:, pl.ds(pl.multiple_of(k * LANES, LANES), LANES)].astype(F32)
        for s in range(STN_DEV):
            rows_ref[s, pl.ds(k, 1), :] = piece[s : s + 1, :]

    own_ref[...] = rows_ref[...].astype(BF16)
    pl.semaphore_wait(barrier, len(near))

    my_rows = pl.ds(pl.multiple_of(me * N1_BLOCK, N1_BLOCK), N1_BLOCK)
    swaps = [
        remote(
            own_ref.at[pl.ds(2 * to, 2), pl.ds(low * HALF, HALF)], pair_ref.at[low, core], pair_send.at[low, to], pair_recv.at[low, core],
            device,
        )
        for low, to, device in others
    ]
    arrivals = [
        remote(own_ref.at[pl.ds(0, 2), pl.ds(0, HALF)], pair_ref.at[low, to], pair_send.at[low, to], pair_recv.at[low, to], device)
        for low, to, device in others
    ]
    if not high:
        kept = remote(
            own_ref.at[pl.ds(2 - 2 * core, 2), pl.ds(0, HALF)], pair_ref.at[0, core], pair_send.at[0, 0], pair_recv.at[0, 0], (stn, mate)
        )
        swaps.append(kept)
        arrivals.append(kept)
        pair_ref[0, core] = own_ref[pl.ds(2 * core, 2), :HALF]
    for copy in swaps:
        copy.start()
    copies = []
    for d, peer in enumerate(line):
        copy = remote(
            own_ref.at[pl.ds(peer // 2, 1)], out_ref.at[pl.ds(0, 1), my_rows], own_send.at[d], own_recv.at[d], (stn, peer)
        )
        copy.start()
        copies.append(copy)
    out_ref[0, my_rows, :] = own_ref[chip]
    out_ref[:, WINDOWS * N1_BLOCK :, :] = jnp.zeros((3, N1_BLOCK, LANES), BF16)
    loads[1].wait()
    for copy in arrivals:
        copy.wait_recv()
    bit = jnp.bitwise_and(partner_smem[0], 1)
    pick_ref[0] = pair_ref[bit]
    pick_ref[1] = pair_ref[1 - bit]
    for cross in range(2):
        for d in range(1 - cross, LINE // 2):
            copy = remote(
                pick_ref.at[cross], land_ref.at[cross, chip], far_send.at[cross, d], far_recv.at[cross, d], (stn ^ cross, column[d])
            )
            copy.start()
            copies.append(copy)
    land_ref[0, chip] = pick_ref[0]
    for copy in copies:
        copy.wait_recv()
    for half in range(2):
        blocks = land_ref[bit if half == 0 else 1 - bit]
        for sender in range(LINE):
            start = sender * N1_BLOCK + half * HALF
            out_ref[1:3, start : start + HALF, :] = blocks[sender // 2, sender % 2]
    for copy in copies + swaps:
        copy.wait_send()
    for copy in fetches:
        copy.wait()


def exchange(high, samples, partner, *consts):
    block = (STN_DEV, N1_BLOCK, LANES)
    half = (2, 2, HALF, LANES)
    anywhere = pl.BlockSpec(memory_space=pl.ANY)
    vmem = pl.BlockSpec(memory_space=pltpu.VMEM)
    return pl.pallas_call(
        functools.partial(exchange_kernel, high, len(consts)),
        name="exchange",
        out_shape=(jax.ShapeDtypeStruct((3, REC_ROWS, LANES), BF16),)
        + tuple(jax.ShapeDtypeStruct(c.shape, c.dtype) for c in consts),
        in_specs=[anywhere] * (2 + len(consts)),
        out_specs=(vmem,) * (1 + len(consts)),
        scratch_shapes=[
            pltpu.SMEM(partner.shape, jnp.int32),
            pltpu.VMEM(samples.shape, BF16),
            pltpu.VMEM(block, F32),
            pltpu.VMEM(block, BF16),
            pltpu.VMEM((2,) + half, BF16),
            pltpu.VMEM((2,) + half, BF16),
            pltpu.VMEM((2, LINE // 2) + half, BF16),
            pltpu.SemaphoreType.DMA((2,)),
            pltpu.SemaphoreType.DMA((len(consts),)),
            pltpu.SemaphoreType.DMA((2, 2)),
            pltpu.SemaphoreType.DMA((2, 2)),
            pltpu.SemaphoreType.DMA((LINE - 1,)),
            pltpu.SemaphoreType.DMA((LINE - 1,)),
            pltpu.SemaphoreType.DMA((2, LINE // 2)),
            pltpu.SemaphoreType.DMA((2, LINE // 2)),
        ],
        compiler_params=pltpu.CompilerParams(collective_id=high, has_side_effects=True),
    )(partner, samples, *consts)


def correlate_kernel(
    sizes_ref, partner_ref, rec_ref, first_ref, twist_ref, second_ref, last_ref, share_ref,
    plain_ref, refined_ref, left_ref, spec_ref, sizes_smem, partner_smem, in_sem,
):
    loads = [
        pltpu.make_async_copy(sizes_ref, sizes_smem, in_sem.at[0]),
        pltpu.make_async_copy(partner_ref, partner_smem, in_sem.at[1]),
    ]
    for copy in loads:
        copy.start()
    cos, sin = twist_ref[:, :LANES], twist_ref[:, LANES:]
    cos2, sin2 = jnp.concatenate([cos, cos], axis=0), jnp.concatenate([sin, sin], axis=0)
    first = first_ref[...]
    second_hi, second_lo = second_ref[:, : 2 * LANES], second_ref[:, 2 * LANES :]
    roots = []
    powers = []
    levels = []
    for s in range(3):
        for j in range(0, WINDOWS, 2):
            one = rec_ref[s, j * N1_BLOCK : (j + 2) * N1_BLOCK, :]
            two = rec_ref[s, (j + 1) * N1_BLOCK : (j + 3) * N1_BLOCK, :]
            both = jnp.concatenate([one, two], axis=1)
            grid = jnp.dot(first, jnp.concatenate([both, both], axis=0), preferred_element_type=F32)
            re = jnp.concatenate([grid[:ROWS, :LANES], grid[:ROWS, LANES:]], axis=0)
            im = jnp.concatenate([grid[ROWS:, :LANES], grid[ROWS:, LANES:]], axis=0)
            re, im = twisted(re, im, cos2, sin2)
            rows = slice((s * WINDOWS + j) * ROWS, (s * WINDOWS + j + 2) * ROWS)
            re_hi, re_lo = halves(re)
            im_hi, im_lo = halves(im)
            left_ref[rows, :] = jnp.concatenate([re_hi, im_hi, re_lo, im_lo], axis=1)
        rows = slice(s * WINDOWS * ROWS, (s + 1) * WINDOWS * ROWS)
        left_hi = left_ref[rows, : 2 * LANES]
        left_lo = left_ref[rows, 2 * LANES :]
        spec_ref[rows, :] = (
            jnp.dot(left_hi, second_hi, preferred_element_type=F32)
            + jnp.dot(left_lo, second_hi, preferred_element_type=F32)
            + jnp.dot(left_hi, second_lo, preferred_element_type=F32)
        )
        power = jnp.zeros((ROWS, LANES), F32)
        for j in range(WINDOWS):
            one = spec_ref[(s * WINDOWS + j) * ROWS : (s * WINDOWS + j + 1) * ROWS, :]
            one = one * one
            power = power + one[:, :LANES] + one[:, LANES:]
        smooth = power
        for shift in (-2, -1, 1, 2):
            smooth = smooth + pltpu.roll(power, shift % ROWS, axis=0)
        level = smooth / 5.0 / WINDOWS + SMALL
        roots.append(1.0 / jnp.sqrt(level))
        powers.append(power)
        levels.append(level)

    auto = powers[0] / levels[0]
    mean = jnp.sum(auto * share_ref[...])
    keep = 1.0 - auto / (mean + SMALL)

    cross = []
    sums = [[jnp.zeros((ROWS, LANES), F32) for _ in range(2)] for _ in range(2)]
    for j in range(WINDOWS):
        source = spec_ref[j * ROWS : (j + 1) * ROWS, :]
        a_re, a_im = source[:, :LANES] * roots[0], source[:, LANES:] * roots[0]
        for b in range(2):
            start = ((b + 1) * WINDOWS + j) * ROWS
            target = spec_ref[start : start + ROWS, :]
            b_re, b_im = target[:, :LANES] * roots[b + 1], target[:, LANES:] * roots[b + 1]
            sums[b][0] = sums[b][0] + (a_re * b_re + a_im * b_im)
            sums[b][1] = sums[b][1] + (a_im * b_re - a_re * b_im)
    for b in range(2):
        plain = jnp.concatenate(sums[b], axis=1)
        cross.append(plain)
        cross.append(plain * jnp.concatenate([keep, keep], axis=1))
    cross = jnp.concatenate(cross, axis=0)
    cross_hi, cross_lo = halves(cross)
    half = (
        jnp.dot(cross_hi, second_hi, preferred_element_type=F32)
        + jnp.dot(cross_lo, second_hi, preferred_element_type=F32)
        + jnp.dot(cross_hi, second_lo, preferred_element_type=F32)
    )
    columns = []
    for i in range(4):
        part = half[i * ROWS : (i + 1) * ROWS]
        re, im = twisted(part[:, :LANES], part[:, LANES:], cos, sin)
        columns.append(jnp.concatenate([re, im], axis=0))
    columns = jnp.concatenate(columns, axis=1)
    col_hi, col_lo = halves(columns)
    lags = jnp.dot(last_ref[...], jnp.concatenate([col_hi, col_hi, col_lo], axis=0), preferred_element_type=F32)

    for copy in loads:
        copy.wait()
    block = lax.axis_index("stn")
    line = lax.axis_index("tm")
    source_live = (line // 2 < sizes_smem[block]).astype(F32)
    other_size = sizes_smem[partner_smem[block]]
    for b in range(2):
        live = source_live * (lax.rem(line, 2) * 2 + b < other_size).astype(F32)
        for kind, ref in enumerate((plain_ref, refined_ref)):
            index = 2 * b + kind
            value = lags[:, index * LANES : (index + 1) * LANES] * live
            for k in range(N1_BLOCK):
                ref[b : b + 1, k * LANES : (k + 1) * LANES] = value[k : k + 1, :]


def correlate(array_sizes, partner, record, *consts):
    out = jax.ShapeDtypeStruct((2, LAGS), F32)
    vmem = pl.BlockSpec(memory_space=pltpu.VMEM)
    return pl.pallas_call(
        correlate_kernel,
        name="correlate",
        out_shape=(out, out),
        in_specs=[pl.BlockSpec(memory_space=pl.ANY)] * 2 + [vmem] * 6,
        out_specs=(vmem, vmem),
        scratch_shapes=[
            pltpu.VMEM((3 * WINDOWS * ROWS, 4 * LANES), BF16),
            pltpu.VMEM((3 * WINDOWS * ROWS, 2 * LANES), F32),
            pltpu.SMEM(array_sizes.shape, jnp.int32),
            pltpu.SMEM(partner.shape, jnp.int32),
            pltpu.SemaphoreType.DMA((2,)),
        ],
    )(array_sizes, partner, record, *consts)


def per_device(samples, array_sizes, partner):
    branches = [functools.partial(exchange, high) for high in range(lax.axis_size("stn") // 2)]
    consts = [jnp.asarray(table) for table in tables()]
    staged = lax.switch(lax.shift_right_logical(partner[0], 1), branches, samples, partner, *consts)
    return correlate(array_sizes, partner, *staged)


def solution(mesh):
    placed = (P("stn", "tm"), P(), P())
    return jax.shard_map(
        per_device,
        mesh=mesh,
        in_specs=placed,
        out_specs=(P(("stn", "tm"), None), P(("stn", "tm"), None)),
        check_vma=False,
    )
```

```python
import functools
import math

import jax
import jax.numpy as jnp
import ml_dtypes
import numpy as np
from jax import lax
from jax.experimental import pallas as pl
from jax.experimental.pallas import tpu as pltpu
from jax.sharding import PartitionSpec as P

LAGS = 4096
SPECTRUM = 8192
WINDOWS = 8
STN_DEV = 4
LINE = 8
LANES = 128
COARSE = 64
HALO = 2
ROWS = 40
N1_BLOCK = LAGS // LANES
HALF = N1_BLOCK // 2
REC_ROWS = (WINDOWS + 1) * N1_BLOCK
SMALL = 1e-06
F32 = jnp.float32
BF16 = jnp.bfloat16


def split_table(table):
    high = table.astype(ml_dtypes.bfloat16)
    low = (table - high.astype(np.float64)).astype(ml_dtypes.bfloat16)
    return high, low


def tables():
    f1 = np.arange(ROWS) - HALO
    n1 = np.arange(COARSE)
    n2 = np.arange(LANES)
    phase = 2.0 * np.pi * (np.outer(f1, n1) % COARSE) / COARSE
    first = np.concatenate([np.cos(phase), -np.sin(phase)], axis=0)
    first = np.concatenate(split_table(first), axis=1)
    phase = 2.0 * np.pi * np.outer(f1, n2) / SPECTRUM
    twist = np.concatenate([np.cos(phase), np.sin(phase)], axis=1).astype(np.float32)
    phase = 2.0 * np.pi * (np.outer(n2, n2) % LANES) / LANES
    cos, sin = np.cos(phase), np.sin(phase)
    second = np.block([[cos, -sin], [sin, cos]])
    second = np.concatenate(split_table(second), axis=1)
    weight = np.where((f1 == 0) | (f1 == COARSE // 2), 1.0, 2.0) * ((f1 >= 0) & (f1 <= COARSE // 2))
    lag1 = np.arange(N1_BLOCK)
    phase = 2.0 * np.pi * (np.outer(lag1, f1) % COARSE) / COARSE
    scale = 1.0 / math.sqrt(SPECTRUM * WINDOWS)
    last = np.concatenate([np.cos(phase) * weight, np.sin(phase) * weight], axis=1) * scale
    high, low = split_table(last)
    last = np.concatenate([high, low, high], axis=1)
    share = np.broadcast_to((weight / SPECTRUM)[:, None], (ROWS, LANES)).astype(np.float32)
    return first, twist, second, last, share


def halves(value):
    high = value.astype(BF16)
    low = (value - high.astype(F32)).astype(BF16)
    return high, low


def twisted(re, im, cos, sin):
    return re * cos + im * sin, im * cos - re * sin


def remote(src, dst, send, recv, device):
    return pltpu.make_async_remote_copy(
        src_ref=src, dst_ref=dst, send_sem=send, recv_sem=recv, device_id=device, device_id_type=pl.DeviceIdType.MESH
    )


def signal(semaphore, device):
    pl.semaphore_signal(semaphore, inc=1, device_id=device, device_id_type=pl.DeviceIdType.MESH)


def exchange_kernel(high, n_tables, partner_ref, samples_ref, *refs):
    tables_in, out_ref, tables_out = refs[:n_tables], refs[n_tables], refs[n_tables + 1 : 2 * n_tables + 1]
    (
        partner_smem, samples_vmem, rows_ref, own_ref, pair_ref, pick_ref, land_ref, in_sem, table_sem, pair_send, pair_recv, own_send, own_recv, far_send,
        far_recv,
    ) = refs[2 * n_tables + 1 :]
    stn = lax.axis_index("stn")
    me = lax.axis_index("tm")
    chip, core = me // 2, lax.rem(me, 2)
    barrier = pltpu.get_barrier_semaphore()
    others = [(low, to, (stn ^ (2 * high + low), 2 * chip + to)) for low in range(2) for to in range(2)]
    line = [lax.rem(me + d, LINE) for d in range(1, LINE)]
    column = [lax.rem(me + 2 * d, LINE) for d in range(LINE // 2)]
    near = [device for _, _, device in others] + [(stn, peer) for peer in line]
    near += [(stn ^ 1, peer) for peer in column]
    for device in near:
        signal(barrier, device)
    loads = [
        pltpu.make_async_copy(samples_ref, samples_vmem, in_sem.at[0]),
        pltpu.make_async_copy(partner_ref, partner_smem, in_sem.at[1]),
    ]
    fetches = [pltpu.make_async_copy(a, b, table_sem.at[i]) for i, (a, b) in enumerate(zip(tables_in, tables_out))]
    for copy in loads + fetches:
        copy.start()
    loads[0].wait()

    @pl.loop(0, N1_BLOCK, unroll=4)
    def _(k):
        piece = samples_vmem[:, pl.ds(pl.multiple_of(k * LANES, LANES), LANES)].astype(F32)
        for s in range(STN_DEV):
            rows_ref[s, pl.ds(k, 1), :] = piece[s : s + 1, :]

    own_ref[...] = rows_ref[...].astype(BF16)
    pl.semaphore_wait(barrier, len(near))

    my_rows = pl.ds(pl.multiple_of(me * N1_BLOCK, N1_BLOCK), N1_BLOCK)
    swaps = [
        remote(
            own_ref.at[pl.ds(2 * to, 2), pl.ds(low * HALF, HALF)], pair_ref.at[low, core], pair_send.at[low, to], pair_recv.at[low, core],
            device,
        )
        for low, to, device in others
    ]
    arrivals = [
        remote(own_ref.at[pl.ds(0, 2), pl.ds(0, HALF)], pair_ref.at[low, to], pair_send.at[low, to], pair_recv.at[low, to], device)
        for low, to, device in others
    ]
    for copy in swaps:
        copy.start()
    copies = []
    for d, peer in enumerate(line):
        copy = remote(
            own_ref.at[pl.ds(peer // 2, 1)], out_ref.at[pl.ds(0, 1), my_rows], own_send.at[d], own_recv.at[d], (stn, peer)
        )
        copy.start()
        copies.append(copy)
    out_ref[0, my_rows, :] = own_ref[chip]
    out_ref[:, WINDOWS * N1_BLOCK :, :] = jnp.zeros((3, N1_BLOCK, LANES), BF16)
    loads[1].wait()
    for copy in arrivals:
        copy.wait_recv()
    bit = jnp.bitwise_and(partner_smem[0], 1)
    pick_ref[0] = pair_ref[bit]
    pick_ref[1] = pair_ref[1 - bit]
    for cross in (1, 0):
        for d in range(1 - cross, LINE // 2):
            copy = remote(
                pick_ref.at[cross], land_ref.at[cross, chip], far_send.at[cross, d], far_recv.at[cross, d], (stn ^ cross, column[d])
            )
            copy.start()
            copies.append(copy)
    land_ref[0, chip] = pick_ref[0]
    for copy in copies:
        copy.wait_recv()
    for half in range(2):
        blocks = land_ref[bit if half == 0 else 1 - bit]
        for sender in range(LINE):
            start = sender * N1_BLOCK + half * HALF
            out_ref[1:3, start : start + HALF, :] = blocks[sender // 2, sender % 2]
    for copy in copies + swaps:
        copy.wait_send()
    for copy in fetches:
        copy.wait()


def exchange(high, samples, partner, *consts):
    block = (STN_DEV, N1_BLOCK, LANES)
    half = (2, 2, HALF, LANES)
    anywhere = pl.BlockSpec(memory_space=pl.ANY)
    vmem = pl.BlockSpec(memory_space=pltpu.VMEM)
    return pl.pallas_call(
        functools.partial(exchange_kernel, high, len(consts)),
        name="exchange",
        out_shape=(jax.ShapeDtypeStruct((3, REC_ROWS, LANES), BF16),)
        + tuple(jax.ShapeDtypeStruct(c.shape, c.dtype) for c in consts),
        in_specs=[anywhere] * (2 + len(consts)),
        out_specs=(vmem,) * (1 + len(consts)),
        scratch_shapes=[
            pltpu.SMEM(partner.shape, jnp.int32),
            pltpu.VMEM(samples.shape, BF16),
            pltpu.VMEM(block, F32),
            pltpu.VMEM(block, BF16),
            pltpu.VMEM((2,) + half, BF16),
            pltpu.VMEM((2,) + half, BF16),
            pltpu.VMEM((2, LINE // 2) + half, BF16),
            pltpu.SemaphoreType.DMA((2,)),
            pltpu.SemaphoreType.DMA((len(consts),)),
            pltpu.SemaphoreType.DMA((2, 2)),
            pltpu.SemaphoreType.DMA((2, 2)),
            pltpu.SemaphoreType.DMA((LINE - 1,)),
            pltpu.SemaphoreType.DMA((LINE - 1,)),
            pltpu.SemaphoreType.DMA((2, LINE // 2)),
            pltpu.SemaphoreType.DMA((2, LINE // 2)),
        ],
        compiler_params=pltpu.CompilerParams(collective_id=high, has_side_effects=True),
    )(partner, samples, *consts)


def direct_kernel(high, n_tables, partner_ref, samples_ref, *refs):
    tables_in, out_ref, tables_out = refs[:n_tables], refs[n_tables], refs[n_tables + 1 : 2 * n_tables + 1]
    (
        partner_smem, samples_vmem, rows_ref, own_ref, pair_ref, in_sem, table_sem, pair_send, pair_recv, own_send, own_recv, far_send,
        far_recv,
    ) = refs[2 * n_tables + 1 :]
    stn = lax.axis_index("stn")
    me = lax.axis_index("tm")
    chip, core = me // 2, lax.rem(me, 2)
    barrier = pltpu.get_barrier_semaphore()
    lows = range(0 if high else 1, 2)
    others = [(low, to, (stn ^ (2 * high + low), 2 * chip + to)) for low in lows for to in range(2)]
    line = [lax.rem(me + d, LINE) for d in range(1, LINE)]
    for device in [device for _, _, device in others] + [(stn, peer) for peer in line]:
        signal(barrier, device)
    loads = [
        pltpu.make_async_copy(samples_ref, samples_vmem, in_sem.at[0]),
        pltpu.make_async_copy(partner_ref, partner_smem, in_sem.at[1]),
    ]
    fetches = [pltpu.make_async_copy(a, b, table_sem.at[i]) for i, (a, b) in enumerate(zip(tables_in, tables_out))]
    for copy in loads + fetches:
        copy.start()
    loads[0].wait()

    @pl.loop(0, N1_BLOCK, unroll=4)
    def _(k):
        piece = samples_vmem[:, pl.ds(pl.multiple_of(k * LANES, LANES), LANES)].astype(F32)
        for s in range(STN_DEV):
            rows_ref[s, pl.ds(k, 1), :] = piece[s : s + 1, :]

    own_ref[...] = rows_ref[...].astype(BF16)
    pl.semaphore_wait(barrier, len(others) + len(line))

    my_rows = pl.ds(pl.multiple_of(me * N1_BLOCK, N1_BLOCK), N1_BLOCK)
    chip_rows = pl.ds(pl.multiple_of(chip * 2 * N1_BLOCK, 2 * N1_BLOCK), 2 * N1_BLOCK)
    core_rows = pl.ds(pl.multiple_of(core * N1_BLOCK, N1_BLOCK), N1_BLOCK)
    swaps = [
        remote(own_ref.at[pl.ds(2 * to, 2)], pair_ref.at[low, :, core_rows], pair_send.at[low, to], pair_recv.at[low, core], device)
        for low, to, device in others
    ]
    arrivals = [
        remote(own_ref.at[pl.ds(0, 2)], pair_ref.at[low, :, pl.ds(to * N1_BLOCK, N1_BLOCK)], pair_send.at[low, to], pair_recv.at[low, to], device)
        for low, to, device in others
    ]
    for copy in swaps:
        copy.start()
    copies = []
    for d, peer in enumerate(line):
        copy = remote(
            own_ref.at[pl.ds(peer // 2, 1)], out_ref.at[pl.ds(0, 1), my_rows], own_send.at[d], own_recv.at[d], (stn, peer)
        )
        copy.start()
        copies.append(copy)
    out_ref[0, my_rows, :] = own_ref[chip]
    out_ref[:, WINDOWS * N1_BLOCK :, :] = jnp.zeros((3, N1_BLOCK, LANES), BF16)
    loads[1].wait()
    for copy in arrivals:
        copy.wait_recv()
    out_ref[1:3, chip_rows, :] = pair_ref[jnp.bitwise_and(partner_smem[0], 1)] if high else pair_ref[1]
    for d in range(LINE // 2 - 1):
        peer = lax.rem(me + 2 * (d + 1), LINE)
        copy = remote(
            out_ref.at[pl.ds(1, 2), chip_rows], out_ref.at[pl.ds(1, 2), chip_rows], far_send.at[d], far_recv.at[d], (stn, peer)
        )
        copy.start()
        copies.append(copy)
    for copy in copies:
        copy.wait_recv()
    for copy in copies + swaps:
        copy.wait_send()
    for copy in fetches:
        copy.wait()


def exchange_direct(high, samples, partner, *consts):
    block = (STN_DEV, N1_BLOCK, LANES)
    anywhere = pl.BlockSpec(memory_space=pl.ANY)
    vmem = pl.BlockSpec(memory_space=pltpu.VMEM)
    return pl.pallas_call(
        functools.partial(direct_kernel, high, len(consts)),
        name="exchange_direct",
        out_shape=(jax.ShapeDtypeStruct((3, REC_ROWS, LANES), BF16),)
        + tuple(jax.ShapeDtypeStruct(c.shape, c.dtype) for c in consts),
        in_specs=[anywhere] * (2 + len(consts)),
        out_specs=(vmem,) * (1 + len(consts)),
        scratch_shapes=[
            pltpu.SMEM(partner.shape, jnp.int32),
            pltpu.VMEM(samples.shape, BF16),
            pltpu.VMEM(block, F32),
            pltpu.VMEM(block, BF16),
            pltpu.VMEM((2, 2, 2 * N1_BLOCK, LANES), BF16),
            pltpu.SemaphoreType.DMA((2,)),
            pltpu.SemaphoreType.DMA((len(consts),)),
            pltpu.SemaphoreType.DMA((2, 2)),
            pltpu.SemaphoreType.DMA((2, 2)),
            pltpu.SemaphoreType.DMA((LINE - 1,)),
            pltpu.SemaphoreType.DMA((LINE - 1,)),
            pltpu.SemaphoreType.DMA((LINE // 2 - 1,)),
            pltpu.SemaphoreType.DMA((LINE // 2 - 1,)),
        ],
        compiler_params=pltpu.CompilerParams(collective_id=high, has_side_effects=True),
    )(partner, samples, *consts)


def correlate_kernel(
    sizes_ref, partner_ref, rec_ref, first_ref, twist_ref, second_ref, last_ref, share_ref,
    plain_ref, refined_ref, left_ref, spec_ref, sizes_smem, partner_smem, in_sem,
):
    loads = [
        pltpu.make_async_copy(sizes_ref, sizes_smem, in_sem.at[0]),
        pltpu.make_async_copy(partner_ref, partner_smem, in_sem.at[1]),
    ]
    for copy in loads:
        copy.start()
    cos, sin = twist_ref[:, :LANES], twist_ref[:, LANES:]
    cos2, sin2 = jnp.concatenate([cos, cos], axis=0), jnp.concatenate([sin, sin], axis=0)
    first = first_ref[...]
    second_hi, second_lo = second_ref[:, : 2 * LANES], second_ref[:, 2 * LANES :]
    roots = []
    powers = []
    levels = []
    for s in range(3):
        for j in range(0, WINDOWS, 2):
            one = rec_ref[s, j * N1_BLOCK : (j + 2) * N1_BLOCK, :]
            two = rec_ref[s, (j + 1) * N1_BLOCK : (j + 3) * N1_BLOCK, :]
            both = jnp.concatenate([one, two], axis=1)
            grid = jnp.dot(first, jnp.concatenate([both, both], axis=0), preferred_element_type=F32)
            re = jnp.concatenate([grid[:ROWS, :LANES], grid[:ROWS, LANES:]], axis=0)
            im = jnp.concatenate([grid[ROWS:, :LANES], grid[ROWS:, LANES:]], axis=0)
            re, im = twisted(re, im, cos2, sin2)
            rows = slice((s * WINDOWS + j) * ROWS, (s * WINDOWS + j + 2) * ROWS)
            re_hi, re_lo = halves(re)
            im_hi, im_lo = halves(im)
            left_ref[rows, :] = jnp.concatenate([re_hi, im_hi, re_lo, im_lo], axis=1)
        rows = slice(s * WINDOWS * ROWS, (s + 1) * WINDOWS * ROWS)
        left_hi = left_ref[rows, : 2 * LANES]
        left_lo = left_ref[rows, 2 * LANES :]
        spec_ref[rows, :] = (
            jnp.dot(left_hi, second_hi, preferred_element_type=F32)
            + jnp.dot(left_lo, second_hi, preferred_element_type=F32)
            + jnp.dot(left_hi, second_lo, preferred_element_type=F32)
        )
        power = jnp.zeros((ROWS, LANES), F32)
        for j in range(WINDOWS):
            one = spec_ref[(s * WINDOWS + j) * ROWS : (s * WINDOWS + j + 1) * ROWS, :]
            one = one * one
            power = power + one[:, :LANES] + one[:, LANES:]
        smooth = power
        for shift in (-2, -1, 1, 2):
            smooth = smooth + pltpu.roll(power, shift % ROWS, axis=0)
        level = smooth / 5.0 / WINDOWS + SMALL
        roots.append(1.0 / jnp.sqrt(level))
        powers.append(power)
        levels.append(level)

    auto = powers[0] / levels[0]
    mean = jnp.sum(auto * share_ref[...])
    keep = 1.0 - auto / (mean + SMALL)

    cross = []
    sums = [[jnp.zeros((ROWS, LANES), F32) for _ in range(2)] for _ in range(2)]
    for j in range(WINDOWS):
        source = spec_ref[j * ROWS : (j + 1) * ROWS, :]
        a_re, a_im = source[:, :LANES] * roots[0], source[:, LANES:] * roots[0]
        for b in range(2):
            start = ((b + 1) * WINDOWS + j) * ROWS
            target = spec_ref[start : start + ROWS, :]
            b_re, b_im = target[:, :LANES] * roots[b + 1], target[:, LANES:] * roots[b + 1]
            sums[b][0] = sums[b][0] + (a_re * b_re + a_im * b_im)
            sums[b][1] = sums[b][1] + (a_im * b_re - a_re * b_im)
    for b in range(2):
        plain = jnp.concatenate(sums[b], axis=1)
        cross.append(plain)
        cross.append(plain * jnp.concatenate([keep, keep], axis=1))
    cross = jnp.concatenate(cross, axis=0)
    cross_hi, cross_lo = halves(cross)
    half = (
        jnp.dot(cross_hi, second_hi, preferred_element_type=F32)
        + jnp.dot(cross_lo, second_hi, preferred_element_type=F32)
        + jnp.dot(cross_hi, second_lo, preferred_element_type=F32)
    )
    columns = []
    for i in range(4):
        part = half[i * ROWS : (i + 1) * ROWS]
        re, im = twisted(part[:, :LANES], part[:, LANES:], cos, sin)
        columns.append(jnp.concatenate([re, im], axis=0))
    columns = jnp.concatenate(columns, axis=1)
    col_hi, col_lo = halves(columns)
    lags = jnp.dot(last_ref[...], jnp.concatenate([col_hi, col_hi, col_lo], axis=0), preferred_element_type=F32)

    for copy in loads:
        copy.wait()
    block = lax.axis_index("stn")
    line = lax.axis_index("tm")
    source_live = (line // 2 < sizes_smem[block]).astype(F32)
    other_size = sizes_smem[partner_smem[block]]
    for b in range(2):
        live = source_live * (lax.rem(line, 2) * 2 + b < other_size).astype(F32)
        for kind, ref in enumerate((plain_ref, refined_ref)):
            index = 2 * b + kind
            value = lags[:, index * LANES : (index + 1) * LANES] * live
            for k in range(N1_BLOCK):
                ref[b : b + 1, k * LANES : (k + 1) * LANES] = value[k : k + 1, :]


def correlate(array_sizes, partner, record, *consts):
    out = jax.ShapeDtypeStruct((2, LAGS), F32)
    vmem = pl.BlockSpec(memory_space=pltpu.VMEM)
    return pl.pallas_call(
        correlate_kernel,
        name="correlate",
        out_shape=(out, out),
        in_specs=[pl.BlockSpec(memory_space=pl.ANY)] * 2 + [vmem] * 6,
        out_specs=(vmem, vmem),
        scratch_shapes=[
            pltpu.VMEM((3 * WINDOWS * ROWS, 4 * LANES), BF16),
            pltpu.VMEM((3 * WINDOWS * ROWS, 2 * LANES), F32),
            pltpu.SMEM(array_sizes.shape, jnp.int32),
            pltpu.SMEM(partner.shape, jnp.int32),
            pltpu.SemaphoreType.DMA((2,)),
        ],
    )(array_sizes, partner, record, *consts)


def per_device(samples, array_sizes, partner):
    near = [high % 8 == 0 for high in range(lax.axis_size("stn") // 2)]
    branches = [functools.partial(exchange_direct if n else exchange, high) for high, n in enumerate(near)]
    consts = [jnp.asarray(table) for table in tables()]
    staged = lax.switch(lax.shift_right_logical(partner[0], 1), branches, samples, partner, *consts)
    return correlate(array_sizes, partner, *staged)


def solution(mesh):
    placed = (P("stn", "tm"), P(), P())
    return jax.shard_map(
        per_device,
        mesh=mesh,
        in_specs=placed,
        out_specs=(P(("stn", "tm"), None), P(("stn", "tm"), None)),
        check_vma=False,
    )
```
